32 devices in a mesh: section: 8 (over z, x), tp: 4 (over y, core).
Axes of the slice: x: 2, y: 2, z: 4, core: 2. Of those that a mesh axis runs over, the one named last changes fastest.
Arguments:
- x_handed: bfloat16 [8, 768, 4096], P('section', None, 'tp'), may hold values from -6 to 6
- cot_handed: bfloat16 [8, 768, 4096], P('section', None, 'tp'), may hold values from -6 to 6
- w_query: bfloat16 [8, 4096, 4096], P('section', None, 'tp'), may hold values from -0.1875 to 0.1875
- key_value_weight: bfloat16 [8, 4096, 1024], P('section', None, 'tp'), may hold values from -0.125 to 0.125
- w_out: bfloat16 [8, 4096, 4096], P('section', 'tp'), may hold values from -0.1875 to 0.1875
- norm_gain: float32 [8, 4096], P('section'), may hold values from 0.1 to 1.9
Outputs:
- layer_out: bfloat16 [8, 768, 4096], P('section', None, 'tp')
- grad_in: bfloat16 [8, 768, 4096], P('section', None, 'tp')
- grad_query: bfloat16 [8, 4096, 4096], P('section', None, 'tp')
- grad_keyval: bfloat16 [8, 4096, 1024], P('section', None, 'tp')
- grad_out: bfloat16 [8, 4096, 4096], P('section', 'tp')
- grad_gain: float32 [8, 4096], P('section')
The draws below stay inside these ranges and needn't reach their ends.
All inputs are finite; a program needn't handle non-finite values.
Results may differ from the reference program's by a relative error of at most 0.03.
Values may be sent and summed in bfloat16 or wider, within the bound.
A program may use at most 128 MiB of HBM per device.

```python
import jax
import jax.numpy as jnp
from jax import lax

MODEL_FEATURES = 4096
HEAD_SIZE = 128
QUERY_HEADS = 32
KEY_VALUE_HEADS = 4
TOKENS = 768
RELAY_SECTIONS = 8
N_TP = 4


def block_levels(rng, dims, cuts, least, top_value):
    factor_of, own = 1.0, jax.random.fold_in(rng, 6)
    for position, parts in cuts:
        draws = jnp.exp(jax.random.uniform(jax.random.fold_in(own, position), (parts,), jnp.float32, least / len(cuts), top_value / len(cuts)))
        factor_of = factor_of * jnp.repeat(draws, dims[position] // parts).reshape([-1 if axis == position else 1 for axis in range(len(dims))])
    return factor_of


def bell_draw(stream_key, dims, spread, limit, pieces=(), kind=jnp.bfloat16):
    array = jax.random.normal(stream_key, dims, jnp.float32) * spread
    if len(pieces) > 0:
        array = block_levels(stream_key, dims, pieces, -0.22, 0.18) * array
    return jnp.clip(array, min=-limit, max=limit).astype(kind)


def setup_inputs(seed: int = 0) -> dict:
    key_of = jax.random.split(jax.random.key(seed), 7)
    return {
        "x_handed": bell_draw(key_of[0], (RELAY_SECTIONS, TOKENS, MODEL_FEATURES), 1.0, 6.0, ((0, 8), (2, 4))),
        "cot_handed": bell_draw(key_of[1], (RELAY_SECTIONS, TOKENS, MODEL_FEATURES), 1.0, 6.0, ((0, 8), (2, 4))),
        "w_query": bell_draw(key_of[2], (RELAY_SECTIONS, MODEL_FEATURES, QUERY_HEADS * HEAD_SIZE), (MODEL_FEATURES // 4) ** -0.5, 0.1875, ((0, 8), (2, 4))),
        "key_value_weight": bell_draw(key_of[3], (RELAY_SECTIONS, MODEL_FEATURES, 2 * KEY_VALUE_HEADS * HEAD_SIZE), (MODEL_FEATURES // 2) ** -0.5, 0.125, ((0, 8), (2, 4))),
        "w_out": bell_draw(key_of[4], (RELAY_SECTIONS, QUERY_HEADS * HEAD_SIZE, MODEL_FEATURES), (QUERY_HEADS * HEAD_SIZE // 4) ** -0.5, 0.1875, ((0, 8), (1, 4))),
        "norm_gain": jnp.clip(1.0 + 0.18 * jax.random.normal(key_of[5], (RELAY_SECTIONS, MODEL_FEATURES), jnp.float32), 0.1, 1.9),
    }


def round_trip(value_rows_full):
    return lax.optimization_barrier(value_rows_full.astype(jnp.bfloat16)).astype(jnp.float32)

def section_pass(operands):
    x_rows, dy_rows, w_q, w_kv, w_o, gain_row = operands
    sequence_length = x_rows.shape[0]
    heads_per_device = QUERY_HEADS // N_TP
    key_value_columns = 2 * KEY_VALUE_HEADS * HEAD_SIZE // N_TP
    query_group_width = QUERY_HEADS // KEY_VALUE_HEADS
    score_scale = HEAD_SIZE ** (-0.5)
    x_float = x_rows.astype(jnp.float32)
    inv_rms = lax.rsqrt(lax.optimization_barrier(jnp.mean(x_float * x_float, axis=-1, keepdims=True)) + 1e-05)
    unit_x = x_float * inv_rms
    normed = (unit_x * gain_row).astype(jnp.bfloat16)
    queries = jnp.dot(normed, w_q, preferred_element_type=jnp.float32).astype(jnp.bfloat16)
    key_value_pairs = jnp.dot(normed, w_kv, preferred_element_type=jnp.float32).astype(jnp.bfloat16)
    query_heads = queries.reshape(sequence_length, QUERY_HEADS, HEAD_SIZE).astype(jnp.float32)
    head_keys = jnp.repeat(key_value_pairs[:, :KEY_VALUE_HEADS * HEAD_SIZE].reshape(sequence_length, KEY_VALUE_HEADS, HEAD_SIZE), query_group_width, axis=1).astype(jnp.float32)
    head_values = jnp.repeat(key_value_pairs[:, KEY_VALUE_HEADS * HEAD_SIZE:].reshape(sequence_length, KEY_VALUE_HEADS, HEAD_SIZE), query_group_width, axis=1).astype(jnp.float32)
    scores = jnp.einsum('shd,thd->hst', query_heads, head_keys) * score_scale
    row_ids = lax.broadcasted_iota(jnp.int32, (sequence_length, sequence_length), 0)
    col_ids = lax.broadcasted_iota(jnp.int32, (sequence_length, sequence_length), 1)
    causal = row_ids >= col_ids
    scores = jnp.where(causal[None], scores, jnp.float32(-1e+30))
    row_max = lax.optimization_barrier(jnp.max(scores, axis=-1, keepdims=True))
    shifted_exp = jnp.exp(scores - row_max)
    attn_probs = shifted_exp / lax.optimization_barrier(jnp.sum(shifted_exp, axis=-1, keepdims=True))
    probs_bf = attn_probs.astype(jnp.bfloat16).astype(jnp.float32)
    attended = jnp.einsum('hst,thd->shd', probs_bf, head_values).astype(jnp.bfloat16)
    attn_flat = attended.reshape(sequence_length, QUERY_HEADS * HEAD_SIZE)
    out_terms = jnp.einsum('sgk,gkd->gsd', attn_flat.reshape(sequence_length, N_TP, heads_per_device * HEAD_SIZE).astype(jnp.float32), w_o.reshape(N_TP, heads_per_device * HEAD_SIZE, MODEL_FEATURES).astype(jnp.float32))
    mixed_rows = lax.optimization_barrier(jnp.sum(round_trip(out_terms), axis=0))
    layer_out = (x_float + mixed_rows).astype(jnp.bfloat16)
    dy_float = dy_rows.astype(jnp.float32)
    grad_out = jnp.einsum('sk,sd->kd', attn_flat.astype(jnp.float32), dy_float).astype(jnp.bfloat16)
    d_attended = jnp.einsum('sd,kd->sk', dy_float, w_o.astype(jnp.float32)).astype(jnp.bfloat16)
    d_att_heads = d_attended.reshape(sequence_length, QUERY_HEADS, HEAD_SIZE).astype(jnp.float32)
    d_probs = jnp.einsum('shd,thd->hst', d_att_heads, head_values)
    row_delta = jnp.einsum('shd,shd->hs', d_att_heads, attended.reshape(sequence_length, QUERY_HEADS, HEAD_SIZE).astype(jnp.float32))
    d_scores = (attn_probs * (d_probs - row_delta[:, :, None]) * score_scale).astype(jnp.bfloat16).astype(jnp.float32)
    d_queries = jnp.einsum('hst,thd->shd', d_scores, head_keys).astype(jnp.bfloat16).reshape(sequence_length, QUERY_HEADS * HEAD_SIZE)
    d_key_heads = jnp.einsum('hst,shd->htd', d_scores, query_heads)
    d_value_heads = jnp.einsum('hst,shd->htd', probs_bf, d_att_heads)

    def group_sum(per_head):
        share_per_device = round_trip(lax.optimization_barrier(jnp.sum(per_head.reshape(N_TP, heads_per_device, sequence_length, HEAD_SIZE), axis=1)))
        share_per_key_value = lax.optimization_barrier(jnp.sum(share_per_device.reshape(KEY_VALUE_HEADS, N_TP // KEY_VALUE_HEADS, sequence_length, HEAD_SIZE), axis=1))
        return jnp.transpose(share_per_key_value, (1, 0, 2)).reshape(sequence_length, KEY_VALUE_HEADS * HEAD_SIZE)
    d_keyvals = jnp.concatenate([group_sum(d_key_heads), group_sum(d_value_heads)], axis=1).astype(jnp.bfloat16)
    normed_float = normed.astype(jnp.float32)
    grad_query = jnp.einsum('sd,sk->dk', normed_float, d_queries.astype(jnp.float32)).astype(jnp.bfloat16)
    grad_keyval = jnp.einsum('sd,sk->dk', normed_float, d_keyvals.astype(jnp.float32)).astype(jnp.bfloat16)
    in_terms = jnp.einsum('sgk,dgk->gsd', d_queries.reshape(sequence_length, N_TP, heads_per_device * HEAD_SIZE).astype(jnp.float32), w_q.reshape(MODEL_FEATURES, N_TP, heads_per_device * HEAD_SIZE).astype(jnp.float32))
    in_terms = in_terms + jnp.einsum('sgk,dgk->gsd', d_keyvals.reshape(sequence_length, N_TP, key_value_columns).astype(jnp.float32), w_kv.reshape(MODEL_FEATURES, N_TP, key_value_columns).astype(jnp.float32))
    d_normed = lax.optimization_barrier(jnp.sum(round_trip(in_terms), axis=0))
    grad_gain = lax.optimization_barrier(jnp.sum(d_normed * unit_x, axis=0))
    d_unit = d_normed * gain_row
    d_input = inv_rms * (d_unit - unit_x * lax.optimization_barrier(jnp.mean(d_unit * unit_x, axis=-1, keepdims=True)))
    grad_in = (dy_float + d_input).astype(jnp.bfloat16)
    return (layer_out, grad_in, grad_query, grad_keyval, grad_out, grad_gain)

def reference(x_handed, cot_handed, w_query, key_value_weight, w_out, norm_gain):
    x_prev = jnp.roll(x_handed, 1, axis=0)
    dy_next = jnp.roll(cot_handed, -1, axis=0)
    results = lax.map(section_pass, (x_prev, dy_next, w_query, key_value_weight, w_out, norm_gain))
    return (results[0], results[1], results[2], results[3], results[4], results[5])
```

```python
import jax
import jax.numpy as jnp
from jax import lax
from jax.experimental import pallas as pl
from jax.experimental.pallas import tpu as pltpu
from jax.sharding import PartitionSpec as P

HEAD_SIZE = 128
QUERY_HEADS = 32
KEY_VALUE_HEADS = 4


def shifted(value, axis, steps):
    count = lax.axis_size(axis)
    pairs = [(source, (source + steps) % count) for source in range(count)]
    return lax.ppermute(value, axis, pairs)


NT = (((1,), (1,)), ((), ()))
TN = (((0,), (0,)), ((), ()))
BLOCK_ROWS = 256


def dot(left, right, dims):
    return lax.dot_general(left, right, dims, preferred_element_type=jnp.float32)


def attend_kernel(q_ref, k_ref, v_ref, out_ref, probs_ref):
    rows = q_ref.shape[0]
    for start in range(0, rows, BLOCK_ROWS):
        stop = start + BLOCK_ROWS
        here = slice(start, stop)
        scores = dot(q_ref[here, :], k_ref[:stop, :], NT) * (HEAD_SIZE ** (-0.5))
        row_ids = lax.broadcasted_iota(jnp.int32, scores.shape, 0) + start
        col_ids = lax.broadcasted_iota(jnp.int32, scores.shape, 1)
        scores = jnp.where(row_ids >= col_ids, scores, jnp.float32(-1e30))
        top = jnp.max(scores, axis=-1, keepdims=True)
        powers = jnp.exp(scores - top)
        probs = powers * (1.0 / jnp.sum(powers, axis=-1, keepdims=True))
        probs = probs.astype(jnp.bfloat16)
        probs_ref[0, here, :stop] = probs
        out_ref[here, :] = jnp.dot(
            probs, v_ref[:stop, :], preferred_element_type=jnp.float32
        ).astype(jnp.bfloat16)


def attend(queries, keys, values):
    rows = queries.shape[0]
    heads = queries.shape[1] // HEAD_SIZE
    column = pl.BlockSpec((rows, HEAD_SIZE), lambda h: (0, h))
    fixed = pl.BlockSpec((rows, HEAD_SIZE), lambda h: (0, 0))
    return pl.pallas_call(
        attend_kernel,
        grid=(heads,),
        in_specs=[column, fixed, fixed],
        out_specs=[column, pl.BlockSpec((1, rows, rows), lambda h: (h, 0, 0))],
        out_shape=[
            jax.ShapeDtypeStruct(queries.shape, jnp.bfloat16),
            jax.ShapeDtypeStruct((heads, rows, rows), jnp.bfloat16),
        ],
        compiler_params=pltpu.CompilerParams(vmem_limit_bytes=40 << 20),
        cost_estimate=pl.CostEstimate(
            flops=16 * heads * rows * rows * HEAD_SIZE,
            bytes_accessed=2 * heads * rows * (rows + 2 * HEAD_SIZE),
            transcendentals=heads * rows * rows,
        ),
    )(queries, keys, values)


def backward_kernel(q_ref, k_ref, v_ref, out_ref, dout_ref, probs_ref, dq_ref, dk_ref, dv_ref):
    rows = q_ref.shape[0]

    @pl.when(pl.program_id(0) == 0)
    def _():
        dk_ref[...] = jnp.zeros_like(dk_ref)
        dv_ref[...] = jnp.zeros_like(dv_ref)

    for start in range(0, rows, BLOCK_ROWS):
        stop = start + BLOCK_ROWS
        here = slice(start, stop)
        d_out = dout_ref[here, :]
        delta = jnp.sum(
            d_out.astype(jnp.float32) * out_ref[here, :].astype(jnp.float32), axis=-1, keepdims=True
        )
        probs = probs_ref[0, here, :stop]
        d_probs = dot(d_out, v_ref[:stop, :], NT)
        d_scores = probs.astype(jnp.float32) * (d_probs - delta) * (HEAD_SIZE ** (-0.5))
        d_scores = d_scores.astype(jnp.bfloat16)
        dq_ref[here, :] = jnp.dot(
            d_scores, k_ref[:stop, :], preferred_element_type=jnp.float32
        ).astype(jnp.bfloat16)
        dk_ref[:stop, :] += dot(d_scores, q_ref[here, :], TN)
        dv_ref[:stop, :] += dot(probs, d_out, TN)


def attend_backward(queries, keys, values, attended, d_attended, probs):
    rows = queries.shape[0]
    heads = queries.shape[1] // HEAD_SIZE
    column = pl.BlockSpec((rows, HEAD_SIZE), lambda h: (0, h))
    fixed = pl.BlockSpec((rows, HEAD_SIZE), lambda h: (0, 0))
    return pl.pallas_call(
        backward_kernel,
        grid=(heads,),
        in_specs=[column, fixed, fixed, column, column,
                  pl.BlockSpec((1, rows, rows), lambda h: (h, 0, 0))],
        out_specs=[column, fixed, fixed],
        out_shape=[
            jax.ShapeDtypeStruct(queries.shape, jnp.bfloat16),
            jax.ShapeDtypeStruct(keys.shape, jnp.float32),
            jax.ShapeDtypeStruct(keys.shape, jnp.float32),
        ],
        compiler_params=pltpu.CompilerParams(vmem_limit_bytes=40 << 20),
        cost_estimate=pl.CostEstimate(
            flops=20 * heads * rows * rows * HEAD_SIZE,
            bytes_accessed=2 * heads * rows * (rows + 4 * HEAD_SIZE),
            transcendentals=0,
        ),
    )(queries, keys, values, attended, d_attended, probs)


def scattered(term, width):
    me = lax.axis_index("tp")
    count = lax.axis_size("tp")
    core_pairs = [(i, i ^ 1) for i in range(count)]
    far_pairs = [(i, i ^ 2) for i in range(count)]
    core, row = me % 2, me // 2
    far, near = 1 - row, row

    def block(r, c):
        return term((2 * r + c) * width)

    far_other = block(far, 1 - core).astype(jnp.bfloat16)
    far_arrived = lax.ppermute(far_other, "tp", core_pairs)
    far_mine = block(far, core)
    far_sum = (far_mine + far_arrived.astype(jnp.float32)).astype(jnp.bfloat16)
    across = lax.ppermute(far_sum, "tp", far_pairs)
    near_other = block(near, 1 - core).astype(jnp.bfloat16)
    near_arrived = lax.ppermute(near_other, "tp", core_pairs)
    near_mine = block(near, core)
    return near_mine + near_arrived.astype(jnp.float32), across


def on_device(x_handed, cot_handed, w_query, key_value_weight, w_out, norm_gain):
    wq_dev = w_query[0]
    wkv_dev = key_value_weight[0]
    wo_dev = w_out[0]
    gain_row = norm_gain[0]
    features = wq_dev.shape[0]
    me = lax.axis_index("tp")
    x_part = shifted(x_handed, "section", 1)[0]
    cot_late, x_part = lax.optimization_barrier((cot_handed, x_part))
    dy_part = shifted(cot_late, "section", -1)[0]
    x_all = lax.all_gather(x_part, "tp", axis=1, tiled=True)
    width = x_part.shape[1]
    mine = me * width
    x_float = x_all.astype(jnp.float32)
    inv_rms = lax.rsqrt(jnp.mean(x_float * x_float, axis=-1, keepdims=True) + 1e-05)
    normed_all = (x_float * inv_rms * gain_row).astype(jnp.bfloat16)
    kv_part = jnp.dot(normed_all, wkv_dev, preferred_element_type=jnp.float32).astype(jnp.bfloat16)
    key_value_pairs = lax.all_gather(kv_part, "tp", axis=1, tiled=True)
    queries = jnp.dot(normed_all, wq_dev, preferred_element_type=jnp.float32).astype(jnp.bfloat16)
    keys = lax.dynamic_slice_in_dim(key_value_pairs, me * HEAD_SIZE, HEAD_SIZE, 1)
    values = lax.dynamic_slice_in_dim(
        key_value_pairs, (KEY_VALUE_HEADS + me) * HEAD_SIZE, HEAD_SIZE, 1
    )
    keys, dy_part = lax.optimization_barrier((keys, dy_part))
    dy_all = lax.all_gather(dy_part, "tp", axis=1, tiled=True)
    attended, probs = attend(queries, keys, values)

    def out_term(first):
        block = lax.dynamic_slice_in_dim(wo_dev, first, width, 1)
        return jnp.dot(attended, block, preferred_element_type=jnp.float32)

    mixed_near, mixed_far = scattered(out_term, width)
    layer_out = (
        x_part.astype(jnp.float32) + mixed_near + mixed_far.astype(jnp.float32)
    ).astype(jnp.bfloat16)
    d_attended = dot(dy_all, wo_dev, NT).astype(jnp.bfloat16)
    d_queries, d_keys, d_values = attend_backward(
        queries, keys, values, attended, d_attended, probs
    )
    pair = jnp.concatenate([d_keys, d_values], axis=1).astype(jnp.bfloat16)
    pairs = lax.all_gather(pair, "tp", axis=0)
    d_keyvals = jnp.concatenate(
        [pairs[g, :, :HEAD_SIZE] for g in range(KEY_VALUE_HEADS)]
        + [pairs[g, :, HEAD_SIZE:] for g in range(KEY_VALUE_HEADS)],
        axis=1,
    )
    kv_width = wkv_dev.shape[1]
    d_kv_mine = lax.dynamic_slice_in_dim(d_keyvals, me * kv_width, kv_width, 1)
    wkv_rows = lax.all_to_all(wkv_dev, "tp", split_axis=0, concat_axis=1, tiled=True)

    def in_term(first):
        block = lax.dynamic_slice_in_dim(wq_dev, first, width, 0)
        return dot(d_queries, block, NT)

    d_near, d_far = scattered(in_term, width)
    grad_out = dot(attended, dy_all, TN).astype(jnp.bfloat16)
    grad_query = dot(normed_all, d_queries, TN).astype(jnp.bfloat16)
    grad_keyval = dot(normed_all, d_kv_mine, TN).astype(jnp.bfloat16)
    from_keyval = dot(d_keyvals, wkv_rows, NT)

    def product(a, b):
        return jnp.sum(a.astype(jnp.float32) * b.astype(jnp.float32), axis=1)

    sums = jnp.concatenate([
        product(grad_query, wq_dev) + product(grad_keyval, wkv_dev),
        product(d_queries, queries) + product(pair, jnp.concatenate([keys, values], axis=1)),
    ])
    sums = lax.psum(sums, "tp")
    grad_gain = sums[:features] / gain_row
    row_mean = (sums[features:] / features)[:, None]
    gain_mine = lax.dynamic_slice_in_dim(gain_row, mine, width, 0)
    unit_mine = x_part.astype(jnp.float32) * inv_rms
    d_unit = (d_near + from_keyval + d_far.astype(jnp.float32)) * gain_mine
    grad_in = (
        dy_part.astype(jnp.float32) + inv_rms * (d_unit - unit_mine * row_mean)
    ).astype(jnp.bfloat16)
    return (
        layer_out[None],
        grad_in[None],
        grad_query[None],
        grad_keyval[None],
        grad_out[None],
        grad_gain[None],
    )


def on_device_any(x_handed, cot_handed, w_query, key_value_weight, w_out, norm_gain):
    x_part = shifted(x_handed, "section", 1)[0]
    dy_part = shifted(cot_handed, "section", -1)[0]
    wq_dev = w_query[0]
    wkv_dev = key_value_weight[0]
    wo_dev = w_out[0]
    gain_row = norm_gain[0]
    heads_per_device = wq_dev.shape[1] // HEAD_SIZE
    score_scale = HEAD_SIZE ** (-0.5)
    x_all = lax.all_gather(x_part, "tp", axis=1, tiled=True)
    sequence_length = x_all.shape[0]
    tok_rows = sequence_length // lax.axis_size("tp")
    row_start = lax.axis_index("tp") * tok_rows
    x_float = x_all.astype(jnp.float32)
    inv_rms = lax.rsqrt(jnp.mean(x_float * x_float, axis=-1, keepdims=True) + 1e-05)
    unit_x = x_float * inv_rms
    normed_all = (unit_x * gain_row).astype(jnp.bfloat16)
    queries = jnp.dot(normed_all, wq_dev, preferred_element_type=jnp.float32).astype(jnp.bfloat16)
    kv_part = jnp.dot(normed_all, wkv_dev, preferred_element_type=jnp.float32).astype(jnp.bfloat16)
    key_value_pairs = lax.all_gather(kv_part, "tp", axis=1, tiled=True)
    key_value_head = lax.axis_index("tp") * heads_per_device // (QUERY_HEADS // KEY_VALUE_HEADS)
    key_rows = lax.dynamic_slice_in_dim(key_value_pairs, key_value_head * HEAD_SIZE, HEAD_SIZE, 1)
    value_rows_full = lax.dynamic_slice_in_dim(
        key_value_pairs, KEY_VALUE_HEADS * HEAD_SIZE + key_value_head * HEAD_SIZE, HEAD_SIZE, 1
    )
    query_heads = queries.reshape(sequence_length, heads_per_device, HEAD_SIZE)
    scores = (
        jnp.einsum("shd,td->hst", query_heads, key_rows, preferred_element_type=jnp.float32)
        * score_scale
    )
    row_ids = lax.broadcasted_iota(jnp.int32, (sequence_length, sequence_length), 0)
    col_ids = lax.broadcasted_iota(jnp.int32, (sequence_length, sequence_length), 1)
    causal = row_ids >= col_ids
    scores = jnp.where(causal[None], scores, jnp.float32(-1e30))
    row_max = jnp.max(scores, axis=-1, keepdims=True)
    shifted_exp = jnp.exp(scores - row_max)
    attn_probs = shifted_exp / jnp.sum(shifted_exp, axis=-1, keepdims=True)
    probs_bf = attn_probs.astype(jnp.bfloat16)
    attended = jnp.einsum(
        "hst,td->shd", probs_bf, value_rows_full, preferred_element_type=jnp.float32
    ).astype(jnp.bfloat16)
    attn_flat = attended.reshape(sequence_length, heads_per_device * HEAD_SIZE)
    out_terms = jnp.dot(attn_flat, wo_dev, preferred_element_type=jnp.float32)
    mixed_part = lax.psum_scatter(
        out_terms.astype(jnp.bfloat16), "tp", scatter_dimension=1, tiled=True
    ).astype(jnp.float32)
    layer_out = (x_part.astype(jnp.float32) + mixed_part).astype(jnp.bfloat16)
    dy_all = lax.all_gather(dy_part, "tp", axis=1, tiled=True)
    grad_out = jnp.einsum(
        "sk,sd->kd", attn_flat, dy_all, preferred_element_type=jnp.float32
    ).astype(jnp.bfloat16)
    d_attended = jnp.einsum("sd,kd->sk", dy_all, wo_dev, preferred_element_type=jnp.float32).astype(
        jnp.bfloat16
    )
    d_att_heads = d_attended.reshape(sequence_length, heads_per_device, HEAD_SIZE)
    d_probs = jnp.einsum(
        "shd,td->hst", d_att_heads, value_rows_full, preferred_element_type=jnp.float32
    )
    row_delta = jnp.einsum(
        "shd,shd->hs", d_att_heads.astype(jnp.float32), attended.astype(jnp.float32)
    )
    d_scores = (attn_probs * (d_probs - row_delta[:, :, None]) * score_scale).astype(jnp.bfloat16)
    d_queries = jnp.einsum("hst,td->shd", d_scores, key_rows, preferred_element_type=jnp.float32)
    d_queries = d_queries.astype(jnp.bfloat16).reshape(
        sequence_length, heads_per_device * HEAD_SIZE
    )
    d_key_rows = jnp.einsum(
        "hst,shd->td", d_scores, query_heads, preferred_element_type=jnp.float32
    )
    value_row_gradient = jnp.einsum(
        "hst,shd->td", probs_bf, d_att_heads, preferred_element_type=jnp.float32
    )
    key_value_contribution = jnp.zeros(
        (sequence_length, 2 * KEY_VALUE_HEADS * HEAD_SIZE), jnp.float32
    )
    key_value_contribution = lax.dynamic_update_slice(
        key_value_contribution, d_key_rows, (jnp.int32(0), key_value_head * HEAD_SIZE)
    )
    key_value_contribution = lax.dynamic_update_slice(
        key_value_contribution,
        value_row_gradient,
        (jnp.int32(0), KEY_VALUE_HEADS * HEAD_SIZE + key_value_head * HEAD_SIZE),
    )
    d_keyvals = lax.psum_scatter(
        key_value_contribution.astype(jnp.bfloat16), "tp", scatter_dimension=1, tiled=True
    )
    grad_query = jnp.einsum(
        "sd,sk->dk", normed_all, d_queries, preferred_element_type=jnp.float32
    ).astype(jnp.bfloat16)
    grad_keyval = jnp.einsum(
        "sd,sk->dk", normed_all, d_keyvals, preferred_element_type=jnp.float32
    ).astype(jnp.bfloat16)
    from_query = jnp.einsum("sk,dk->sd", d_queries, wq_dev, preferred_element_type=jnp.float32)
    from_keyval = jnp.einsum("sk,dk->sd", d_keyvals, wkv_dev, preferred_element_type=jnp.float32)
    d_normed = lax.psum_scatter(
        (from_query + from_keyval).astype(jnp.bfloat16), "tp", scatter_dimension=0, tiled=True
    ).astype(jnp.float32)
    unit_rows = lax.dynamic_slice_in_dim(unit_x, row_start, tok_rows, 0)
    inv_rows = lax.dynamic_slice_in_dim(inv_rms, row_start, tok_rows, 0)
    dy_rows = lax.dynamic_slice_in_dim(dy_all, row_start, tok_rows, 0).astype(jnp.float32)
    gain_local = jnp.sum(d_normed * unit_rows, axis=0)
    grad_gain = lax.psum(gain_local, "tp")
    d_unit = d_normed * gain_row
    d_input = inv_rows * (d_unit - unit_rows * jnp.mean(d_unit * unit_rows, axis=-1, keepdims=True))
    grad_rows = (dy_rows + d_input).astype(jnp.bfloat16)
    grad_in = lax.all_to_all(grad_rows, "tp", split_axis=1, concat_axis=0, tiled=True)
    return (
        layer_out[None],
        grad_in[None],
        grad_query[None],
        grad_keyval[None],
        grad_out[None],
        grad_gain[None],
    )


def solution(mesh):
    return jax.shard_map(
        on_device if mesh.shape["tp"] == KEY_VALUE_HEADS else on_device_any,
        mesh=mesh,
        in_specs=(
            P("section", None, "tp"),
            P("section", None, "tp"),
            P("section", None, "tp"),
            P("section", None, "tp"),
            P("section", "tp", None),
            P("section", None),
        ),
        out_specs=(
            P("section", None, "tp"),
            P("section", None, "tp"),
            P("section", None, "tp"),
            P("section", None, "tp"),
            P("section", "tp", None),
            P("section", None),
        ),
        check_vma=False,
    )
```

```python
import jax
import jax.numpy as jnp
from jax import lax
from jax.experimental import pallas as pl
from jax.experimental.pallas import tpu as pltpu
from jax.sharding import PartitionSpec as P

HEAD_SIZE = 128
QUERY_HEADS = 32
KEY_VALUE_HEADS = 4


def shifted(value, axis, steps):
    count = lax.axis_size(axis)
    pairs = [(source, (source + steps) % count) for source in range(count)]
    return lax.ppermute(value, axis, pairs)


NT = (((1,), (1,)), ((), ()))
TN = (((0,), (0,)), ((), ()))
BLOCK_ROWS = 256


def dot(left, right, dims):
    return lax.dot_general(left, right, dims, preferred_element_type=jnp.float32)


def attend_kernel(q_ref, k_ref, v_ref, out_ref, probs_ref):
    rows = q_ref.shape[0]
    for start in range(0, rows, BLOCK_ROWS):
        stop = start + BLOCK_ROWS
        here = slice(start, stop)
        scores = dot(q_ref[here, :], k_ref[:stop, :], NT) * (HEAD_SIZE ** (-0.5))
        row_ids = lax.broadcasted_iota(jnp.int32, scores.shape, 0) + start
        col_ids = lax.broadcasted_iota(jnp.int32, scores.shape, 1)
        scores = jnp.where(row_ids >= col_ids, scores, jnp.float32(-1e30))
        top = jnp.max(scores, axis=-1, keepdims=True)
        powers = jnp.exp(scores - top)
        probs = powers * (1.0 / jnp.sum(powers, axis=-1, keepdims=True))
        probs = probs.astype(jnp.bfloat16)
        probs_ref[0, here, :stop] = probs
        out_ref[here, :] = jnp.dot(
            probs, v_ref[:stop, :], preferred_element_type=jnp.float32
        ).astype(jnp.bfloat16)


def attend(queries, keys, values):
    rows = queries.shape[0]
    heads = queries.shape[1] // HEAD_SIZE
    column = pl.BlockSpec((rows, HEAD_SIZE), lambda h: (0, h))
    fixed = pl.BlockSpec((rows, HEAD_SIZE), lambda h: (0, 0))
    return pl.pallas_call(
        attend_kernel,
        grid=(heads,),
        in_specs=[column, fixed, fixed],
        out_specs=[column, pl.BlockSpec((1, rows, rows), lambda h: (h, 0, 0))],
        out_shape=[
            jax.ShapeDtypeStruct(queries.shape, jnp.bfloat16),
            jax.ShapeDtypeStruct((heads, rows, rows), jnp.bfloat16),
        ],
        compiler_params=pltpu.CompilerParams(vmem_limit_bytes=40 << 20),
        cost_estimate=pl.CostEstimate(
            flops=16 * heads * rows * rows * HEAD_SIZE,
            bytes_accessed=2 * heads * rows * (rows + 2 * HEAD_SIZE),
            transcendentals=heads * rows * rows,
        ),
    )(queries, keys, values)


def backward_kernel(q_ref, k_ref, v_ref, out_ref, dout_ref, probs_ref, dq_ref, dk_ref, dv_ref):
    rows = q_ref.shape[0]

    @pl.when(pl.program_id(0) == 0)
    def _():
        dk_ref[...] = jnp.zeros_like(dk_ref)
        dv_ref[...] = jnp.zeros_like(dv_ref)

    for start in range(0, rows, BLOCK_ROWS):
        stop = start + BLOCK_ROWS
        here = slice(start, stop)
        d_out = dout_ref[here, :]
        delta = jnp.sum(
            d_out.astype(jnp.float32) * out_ref[here, :].astype(jnp.float32), axis=-1, keepdims=True
        )
        probs = probs_ref[0, here, :stop]
        d_probs = dot(d_out, v_ref[:stop, :], NT)
        d_scores = probs.astype(jnp.float32) * (d_probs - delta) * (HEAD_SIZE ** (-0.5))
        d_scores = d_scores.astype(jnp.bfloat16)
        dq_ref[here, :] = jnp.dot(
            d_scores, k_ref[:stop, :], preferred_element_type=jnp.float32
        ).astype(jnp.bfloat16)
        dk_ref[:stop, :] += dot(d_scores, q_ref[here, :], TN)
        dv_ref[:stop, :] += dot(probs, d_out, TN)


def attend_backward(queries, keys, values, attended, d_attended, probs):
    rows = queries.shape[0]
    heads = queries.shape[1] // HEAD_SIZE
    column = pl.BlockSpec((rows, HEAD_SIZE), lambda h: (0, h))
    fixed = pl.BlockSpec((rows, HEAD_SIZE), lambda h: (0, 0))
    return pl.pallas_call(
        backward_kernel,
        grid=(heads,),
        in_specs=[column, fixed, fixed, column, column,
                  pl.BlockSpec((1, rows, rows), lambda h: (h, 0, 0))],
        out_specs=[column, fixed, fixed],
        out_shape=[
            jax.ShapeDtypeStruct(queries.shape, jnp.bfloat16),
            jax.ShapeDtypeStruct(keys.shape, jnp.float32),
            jax.ShapeDtypeStruct(keys.shape, jnp.float32),
        ],
        compiler_params=pltpu.CompilerParams(vmem_limit_bytes=40 << 20),
        cost_estimate=pl.CostEstimate(
            flops=20 * heads * rows * rows * HEAD_SIZE,
            bytes_accessed=2 * heads * rows * (rows + 4 * HEAD_SIZE),
            transcendentals=0,
        ),
    )(queries, keys, values, attended, d_attended, probs)


def scattered(term, width):
    me = lax.axis_index("tp")
    count = lax.axis_size("tp")
    core_pairs = [(i, i ^ 1) for i in range(count)]
    far_pairs = [(i, i ^ 2) for i in range(count)]
    core, row = me % 2, me // 2
    far, near = 1 - row, row

    def block(r, c):
        return term((2 * r + c) * width)

    far_other = block(far, 1 - core).astype(jnp.bfloat16)
    far_arrived = lax.ppermute(far_other, "tp", core_pairs)
    far_mine = block(far, core)
    far_sum = (far_mine + far_arrived.astype(jnp.float32)).astype(jnp.bfloat16)
    across = lax.ppermute(far_sum, "tp", far_pairs)
    near_other = block(near, 1 - core).astype(jnp.bfloat16)
    near_arrived = lax.ppermute(near_other, "tp", core_pairs)
    near_mine = block(near, core)
    return near_mine + near_arrived.astype(jnp.float32), across


def on_device(x_handed, cot_handed, w_query, key_value_weight, w_out, norm_gain):
    wq_dev = w_query[0]
    wkv_dev = key_value_weight[0]
    wo_dev = w_out[0]
    gain_row = norm_gain[0]
    features = wq_dev.shape[0]
    me = lax.axis_index("tp")
    x_part = shifted(x_handed, "section", 1)[0]
    dy_part = shifted(cot_handed, "section", -1)[0]
    x_all = lax.all_gather(x_part, "tp", axis=1, tiled=True)
    x_all, dy_part = lax.optimization_barrier((x_all, dy_part))
    width = x_part.shape[1]
    mine = me * width
    x_float = x_all.astype(jnp.float32)
    inv_rms = lax.rsqrt(jnp.mean(x_float * x_float, axis=-1, keepdims=True) + 1e-05)
    normed_all = (x_float * inv_rms * gain_row).astype(jnp.bfloat16)
    kv_part = jnp.dot(normed_all, wkv_dev, preferred_element_type=jnp.float32).astype(jnp.bfloat16)
    key_value_pairs = lax.all_gather(kv_part, "tp", axis=1, tiled=True)
    queries = jnp.dot(normed_all, wq_dev, preferred_element_type=jnp.float32).astype(jnp.bfloat16)
    keys = lax.dynamic_slice_in_dim(key_value_pairs, me * HEAD_SIZE, HEAD_SIZE, 1)
    values = lax.dynamic_slice_in_dim(
        key_value_pairs, (KEY_VALUE_HEADS + me) * HEAD_SIZE, HEAD_SIZE, 1
    )
    keys, dy_part = lax.optimization_barrier((keys, dy_part))
    dy_all = lax.all_gather(dy_part, "tp", axis=1, tiled=True)
    attended, probs = attend(queries, keys, values)

    def out_term(first):
        block = lax.dynamic_slice_in_dim(wo_dev, first, width, 1)
        return jnp.dot(attended, block, preferred_element_type=jnp.float32)

    mixed_near, mixed_far = scattered(out_term, width)
    layer_out = (
        x_part.astype(jnp.float32) + mixed_near + mixed_far.astype(jnp.float32)
    ).astype(jnp.bfloat16)
    d_attended = dot(dy_all, wo_dev, NT).astype(jnp.bfloat16)
    d_queries, d_keys, d_values = attend_backward(
        queries, keys, values, attended, d_attended, probs
    )
    pair = jnp.concatenate([d_keys, d_values], axis=1).astype(jnp.bfloat16)
    pairs = lax.all_gather(pair, "tp", axis=1, tiled=True)
    kv_width = wkv_dev.shape[1]
    half = KEY_VALUE_HEADS // 2
    first_kv = 2 * HEAD_SIZE * half * (me % 2) + HEAD_SIZE * (me // 2)
    d_kv_mine = jnp.concatenate(
        [
            lax.dynamic_slice_in_dim(pairs, first_kv + 2 * HEAD_SIZE * g, HEAD_SIZE, 1)
            for g in range(half)
        ],
        axis=1,
    )
    grad_query = dot(normed_all, d_queries, TN).astype(jnp.bfloat16)
    d_kv_mine, d_queries, grad_query = lax.optimization_barrier((d_kv_mine, d_queries, grad_query))

    def in_term(first):
        block = lax.dynamic_slice_in_dim(wq_dev, first, width, 0)
        kv_block = lax.dynamic_slice_in_dim(wkv_dev, first, width, 0)
        return dot(d_queries, block, NT) + dot(d_kv_mine, kv_block, NT)

    d_near, d_far = scattered(in_term, width)
    grad_out = dot(attended, dy_all, TN).astype(jnp.bfloat16)
    grad_keyval = dot(normed_all, d_kv_mine, TN).astype(jnp.bfloat16)

    def product(a, b):
        return jnp.sum(a.astype(jnp.float32) * b.astype(jnp.float32), axis=1)

    row_dot = product(d_queries, queries) + product(
        pair, jnp.concatenate([keys, values], axis=1)
    )
    row_dot = jnp.sum(lax.all_gather(row_dot, "tp"), axis=0)
    row_mean = (row_dot / features)[:, None]
    gain_mine = lax.dynamic_slice_in_dim(gain_row, mine, width, 0)
    unit_mine = x_part.astype(jnp.float32) * inv_rms
    d_normed = d_near + d_far.astype(jnp.float32)
    grad_gain = lax.all_gather(jnp.sum(d_normed * unit_mine, axis=0), "tp", tiled=True)
    d_unit = d_normed * gain_mine
    grad_in = (
        dy_part.astype(jnp.float32) + inv_rms * (d_unit - unit_mine * row_mean)
    ).astype(jnp.bfloat16)
    return (
        layer_out[None],
        grad_in[None],
        grad_query[None],
        grad_keyval[None],
        grad_out[None],
        grad_gain[None],
    )


def on_device_any(x_handed, cot_handed, w_query, key_value_weight, w_out, norm_gain):
    x_part = shifted(x_handed, "section", 1)[0]
    dy_part = shifted(cot_handed, "section", -1)[0]
    wq_dev = w_query[0]
    wkv_dev = key_value_weight[0]
    wo_dev = w_out[0]
    gain_row = norm_gain[0]
    heads_per_device = wq_dev.shape[1] // HEAD_SIZE
    score_scale = HEAD_SIZE ** (-0.5)
    x_all = lax.all_gather(x_part, "tp", axis=1, tiled=True)
    sequence_length = x_all.shape[0]
    tok_rows = sequence_length // lax.axis_size("tp")
    row_start = lax.axis_index("tp") * tok_rows
    x_float = x_all.astype(jnp.float32)
    inv_rms = lax.rsqrt(jnp.mean(x_float * x_float, axis=-1, keepdims=True) + 1e-05)
    unit_x = x_float * inv_rms
    normed_all = (unit_x * gain_row).astype(jnp.bfloat16)
    queries = jnp.dot(normed_all, wq_dev, preferred_element_type=jnp.float32).astype(jnp.bfloat16)
    kv_part = jnp.dot(normed_all, wkv_dev, preferred_element_type=jnp.float32).astype(jnp.bfloat16)
    key_value_pairs = lax.all_gather(kv_part, "tp", axis=1, tiled=True)
    key_value_head = lax.axis_index("tp") * heads_per_device // (QUERY_HEADS // KEY_VALUE_HEADS)
    key_rows = lax.dynamic_slice_in_dim(key_value_pairs, key_value_head * HEAD_SIZE, HEAD_SIZE, 1)
    value_rows_full = lax.dynamic_slice_in_dim(
        key_value_pairs, KEY_VALUE_HEADS * HEAD_SIZE + key_value_head * HEAD_SIZE, HEAD_SIZE, 1
    )
    query_heads = queries.reshape(sequence_length, heads_per_device, HEAD_SIZE)
    scores = (
        jnp.einsum("shd,td->hst", query_heads, key_rows, preferred_element_type=jnp.float32)
        * score_scale
    )
    row_ids = lax.broadcasted_iota(jnp.int32, (sequence_length, sequence_length), 0)
    col_ids = lax.broadcasted_iota(jnp.int32, (sequence_length, sequence_length), 1)
    causal = row_ids >= col_ids
    scores = jnp.where(causal[None], scores, jnp.float32(-1e30))
    row_max = jnp.max(scores, axis=-1, keepdims=True)
    shifted_exp = jnp.exp(scores - row_max)
    attn_probs = shifted_exp / jnp.sum(shifted_exp, axis=-1, keepdims=True)
    probs_bf = attn_probs.astype(jnp.bfloat16)
    attended = jnp.einsum(
        "hst,td->shd", probs_bf, value_rows_full, preferred_element_type=jnp.float32
    ).astype(jnp.bfloat16)
    attn_flat = attended.reshape(sequence_length, heads_per_device * HEAD_SIZE)
    out_terms = jnp.dot(attn_flat, wo_dev, preferred_element_type=jnp.float32)
    mixed_part = lax.psum_scatter(
        out_terms.astype(jnp.bfloat16), "tp", scatter_dimension=1, tiled=True
    ).astype(jnp.float32)
    layer_out = (x_part.astype(jnp.float32) + mixed_part).astype(jnp.bfloat16)
    dy_all = lax.all_gather(dy_part, "tp", axis=1, tiled=True)
    grad_out = jnp.einsum(
        "sk,sd->kd", attn_flat, dy_all, preferred_element_type=jnp.float32
    ).astype(jnp.bfloat16)
    d_attended = jnp.einsum("sd,kd->sk", dy_all, wo_dev, preferred_element_type=jnp.float32).astype(
        jnp.bfloat16
    )
    d_att_heads = d_attended.reshape(sequence_length, heads_per_device, HEAD_SIZE)
    d_probs = jnp.einsum(
        "shd,td->hst", d_att_heads, value_rows_full, preferred_element_type=jnp.float32
    )
    row_delta = jnp.einsum(
        "shd,shd->hs", d_att_heads.astype(jnp.float32), attended.astype(jnp.float32)
    )
    d_scores = (attn_probs * (d_probs - row_delta[:, :, None]) * score_scale).astype(jnp.bfloat16)
    d_queries = jnp.einsum("hst,td->shd", d_scores, key_rows, preferred_element_type=jnp.float32)
    d_queries = d_queries.astype(jnp.bfloat16).reshape(
        sequence_length, heads_per_device * HEAD_SIZE
    )
    d_key_rows = jnp.einsum(
        "hst,shd->td", d_scores, query_heads, preferred_element_type=jnp.float32
    )
    value_row_gradient = jnp.einsum(
        "hst,shd->td", probs_bf, d_att_heads, preferred_element_type=jnp.float32
    )
    key_value_contribution = jnp.zeros(
        (sequence_length, 2 * KEY_VALUE_HEADS * HEAD_SIZE), jnp.float32
    )
    key_value_contribution = lax.dynamic_update_slice(
        key_value_contribution, d_key_rows, (jnp.int32(0), key_value_head * HEAD_SIZE)
    )
    key_value_contribution = lax.dynamic_update_slice(
        key_value_contribution,
        value_row_gradient,
        (jnp.int32(0), KEY_VALUE_HEADS * HEAD_SIZE + key_value_head * HEAD_SIZE),
    )
    d_keyvals = lax.psum_scatter(
        key_value_contribution.astype(jnp.bfloat16), "tp", scatter_dimension=1, tiled=True
    )
    grad_query = jnp.einsum(
        "sd,sk->dk", normed_all, d_queries, preferred_element_type=jnp.float32
    ).astype(jnp.bfloat16)
    grad_keyval = jnp.einsum(
        "sd,sk->dk", normed_all, d_keyvals, preferred_element_type=jnp.float32
    ).astype(jnp.bfloat16)
    from_query = jnp.einsum("sk,dk->sd", d_queries, wq_dev, preferred_element_type=jnp.float32)
    from_keyval = jnp.einsum("sk,dk->sd", d_keyvals, wkv_dev, preferred_element_type=jnp.float32)
    d_normed = lax.psum_scatter(
        (from_query + from_keyval).astype(jnp.bfloat16), "tp", scatter_dimension=0, tiled=True
    ).astype(jnp.float32)
    unit_rows = lax.dynamic_slice_in_dim(unit_x, row_start, tok_rows, 0)
    inv_rows = lax.dynamic_slice_in_dim(inv_rms, row_start, tok_rows, 0)
    dy_rows = lax.dynamic_slice_in_dim(dy_all, row_start, tok_rows, 0).astype(jnp.float32)
    gain_local = jnp.sum(d_normed * unit_rows, axis=0)
    grad_gain = lax.psum(gain_local, "tp")
    d_unit = d_normed * gain_row
    d_input = inv_rows * (d_unit - unit_rows * jnp.mean(d_unit * unit_rows, axis=-1, keepdims=True))
    grad_rows = (dy_rows + d_input).astype(jnp.bfloat16)
    grad_in = lax.all_to_all(grad_rows, "tp", split_axis=1, concat_axis=0, tiled=True)
    return (
        layer_out[None],
        grad_in[None],
        grad_query[None],
        grad_keyval[None],
        grad_out[None],
        grad_gain[None],
    )


def solution(mesh):
    return jax.shard_map(
        on_device if mesh.shape["tp"] == KEY_VALUE_HEADS else on_device_any,
        mesh=mesh,
        in_specs=(
            P("section", None, "tp"),
            P("section", None, "tp"),
            P("section", None, "tp"),
            P("section", None, "tp"),
            P("section", "tp", None),
            P("section", None),
        ),
        out_specs=(
            P("section", None, "tp"),
            P("section", None, "tp"),
            P("section", None, "tp"),
            P("section", None, "tp"),
            P("section", "tp", None),
            P("section", None),
        ),
        check_vma=False,
    )
```

```python
import jax
import jax.numpy as jnp
from jax import lax
from jax.experimental import pallas as pl
from jax.experimental.pallas import tpu as pltpu
from jax.sharding import PartitionSpec as P

HEAD_SIZE = 128
QUERY_HEADS = 32
KEY_VALUE_HEADS = 4


def shifted(value, axis, steps):
    count = lax.axis_size(axis)
    pairs = [(source, (source + steps) % count) for source in range(count)]
    return lax.ppermute(value, axis, pairs)


NT = (((1,), (1,)), ((), ()))
TN = (((0,), (0,)), ((), ()))
BLOCK_ROWS = 256


def dot(left, right, dims):
    return lax.dot_general(left, right, dims, preferred_element_type=jnp.float32)


def attend_kernel(q_ref, k_ref, v_ref, out_ref, probs_ref):
    rows = q_ref.shape[0]
    for start in range(0, rows, BLOCK_ROWS):
        stop = start + BLOCK_ROWS
        here = slice(start, stop)
        scores = dot(q_ref[here, :], k_ref[:stop, :], NT) * (HEAD_SIZE ** (-0.5))
        row_ids = lax.broadcasted_iota(jnp.int32, scores.shape, 0) + start
        col_ids = lax.broadcasted_iota(jnp.int32, scores.shape, 1)
        scores = jnp.where(row_ids >= col_ids, scores, jnp.float32(-1e30))
        top = jnp.max(scores, axis=-1, keepdims=True)
        powers = jnp.exp(scores - top)
        probs = powers * (1.0 / jnp.sum(powers, axis=-1, keepdims=True))
        probs = probs.astype(jnp.bfloat16)
        probs_ref[0, here, :stop] = probs
        out_ref[here, :] = jnp.dot(
            probs, v_ref[:stop, :], preferred_element_type=jnp.float32
        ).astype(jnp.bfloat16)


def attend(queries, keys, values):
    rows = queries.shape[0]
    heads = queries.shape[1] // HEAD_SIZE
    column = pl.BlockSpec((rows, HEAD_SIZE), lambda h: (0, h))
    fixed = pl.BlockSpec((rows, HEAD_SIZE), lambda h: (0, 0))
    return pl.pallas_call(
        attend_kernel,
        grid=(heads,),
        in_specs=[column, fixed, fixed],
        out_specs=[column, pl.BlockSpec((1, rows, rows), lambda h: (h, 0, 0))],
        out_shape=[
            jax.ShapeDtypeStruct(queries.shape, jnp.bfloat16),
            jax.ShapeDtypeStruct((heads, rows, rows), jnp.bfloat16),
        ],
        compiler_params=pltpu.CompilerParams(vmem_limit_bytes=40 << 20),
        cost_estimate=pl.CostEstimate(
            flops=16 * heads * rows * rows * HEAD_SIZE,
            bytes_accessed=2 * heads * rows * (rows + 2 * HEAD_SIZE),
            transcendentals=heads * rows * rows,
        ),
    )(queries, keys, values)


def backward_kernel(q_ref, k_ref, v_ref, out_ref, dout_ref, probs_ref, dq_ref, dk_ref, dv_ref):
    rows = q_ref.shape[0]

    @pl.when(pl.program_id(0) == 0)
    def _():
        dk_ref[...] = jnp.zeros_like(dk_ref)
        dv_ref[...] = jnp.zeros_like(dv_ref)

    for start in range(0, rows, BLOCK_ROWS):
        stop = start + BLOCK_ROWS
        here = slice(start, stop)
        d_out = dout_ref[here, :]
        delta = jnp.sum(
            d_out.astype(jnp.float32) * out_ref[here, :].astype(jnp.float32), axis=-1, keepdims=True
        )
        probs = probs_ref[0, here, :stop]
        d_probs = dot(d_out, v_ref[:stop, :], NT)
        d_scores = probs.astype(jnp.float32) * (d_probs - delta) * (HEAD_SIZE ** (-0.5))
        d_scores = d_scores.astype(jnp.bfloat16)
        dq_ref[here, :] = jnp.dot(
            d_scores, k_ref[:stop, :], preferred_element_type=jnp.float32
        ).astype(jnp.bfloat16)
        dk_ref[:stop, :] += dot(d_scores, q_ref[here, :], TN)
        dv_ref[:stop, :] += dot(probs, d_out, TN)


def attend_backward(queries, keys, values, attended, d_attended, probs):
    rows = queries.shape[0]
    heads = queries.shape[1] // HEAD_SIZE
    column = pl.BlockSpec((rows, HEAD_SIZE), lambda h: (0, h))
    fixed = pl.BlockSpec((rows, HEAD_SIZE), lambda h: (0, 0))
    return pl.pallas_call(
        backward_kernel,
        grid=(heads,),
        in_specs=[column, fixed, fixed, column, column,
                  pl.BlockSpec((1, rows, rows), lambda h: (h, 0, 0))],
        out_specs=[column, fixed, fixed],
        out_shape=[
            jax.ShapeDtypeStruct(queries.shape, jnp.bfloat16),
            jax.ShapeDtypeStruct(keys.shape, jnp.float32),
            jax.ShapeDtypeStruct(keys.shape, jnp.float32),
        ],
        compiler_params=pltpu.CompilerParams(vmem_limit_bytes=40 << 20),
        cost_estimate=pl.CostEstimate(
            flops=20 * heads * rows * rows * HEAD_SIZE,
            bytes_accessed=2 * heads * rows * (rows + 4 * HEAD_SIZE),
            transcendentals=0,
        ),
    )(queries, keys, values, attended, d_attended, probs)


def scattered(term, width, operands):
    me = lax.axis_index("tp")
    count = lax.axis_size("tp")
    core_pairs = [(i, i ^ 1) for i in range(count)]
    far_pairs = [(i, i ^ 2) for i in range(count)]
    core, row = me % 2, me // 2
    far, near = 1 - row, row

    def block(r, c):
        return term((2 * r + c) * width, *operands)

    far_other = block(far, 1 - core).astype(jnp.bfloat16)
    far_arrived = lax.ppermute(far_other, "tp", core_pairs)
    far_mine = block(far, core)
    far_sum = (far_mine + far_arrived.astype(jnp.float32)).astype(jnp.bfloat16)
    far_sum, operands = lax.optimization_barrier((far_sum, operands))
    across = lax.ppermute(far_sum, "tp", far_pairs)
    near_other = block(near, 1 - core).astype(jnp.bfloat16)
    near_arrived = lax.ppermute(near_other, "tp", core_pairs)
    near_mine = block(near, core)
    return near_mine + near_arrived.astype(jnp.float32), across, operands


def on_device(x_handed, cot_handed, w_query, key_value_weight, w_out, norm_gain):
    wq_dev = w_query[0]
    wkv_dev = key_value_weight[0]
    wo_dev = w_out[0]
    gain_row = norm_gain[0]
    features = wq_dev.shape[0]
    me = lax.axis_index("tp")
    x_part = shifted(x_handed, "section", 1)[0]
    dy_part = shifted(cot_handed, "section", -1)[0]
    x_all = lax.all_gather(x_part, "tp", axis=1, tiled=True)
    x_all, dy_part = lax.optimization_barrier((x_all, dy_part))
    width = x_part.shape[1]
    mine = me * width
    x_float = x_all.astype(jnp.float32)
    inv_rms = lax.rsqrt(jnp.mean(x_float * x_float, axis=-1, keepdims=True) + 1e-05)
    normed_all = (x_float * inv_rms * gain_row).astype(jnp.bfloat16)
    kv_part = jnp.dot(normed_all, wkv_dev, preferred_element_type=jnp.float32).astype(jnp.bfloat16)
    low, high = kv_part[:, :HEAD_SIZE], kv_part[:, HEAD_SIZE:]
    edge = (me == 0) | (me == KEY_VALUE_HEADS - 1)
    first_in = lax.ppermute(
        jnp.where(edge, high, low), "tp", [(0, 1), (1, 2), (2, 0), (3, 3)]
    )
    second_in = lax.ppermute(
        jnp.where(edge, low, high), "tp", [(0, 0), (1, 3), (2, 1), (3, 2)]
    )
    queries = jnp.dot(normed_all, wq_dev, preferred_element_type=jnp.float32).astype(jnp.bfloat16)
    keys = jnp.where(edge, second_in, first_in)
    values = jnp.where(edge, first_in, second_in)
    dy_all = lax.all_gather(dy_part, "tp", axis=1, tiled=True)
    attended, probs = attend(queries, keys, values)

    def out_term(first, attended):
        block = lax.dynamic_slice_in_dim(wo_dev, first, width, 1)
        return jnp.dot(attended, block, preferred_element_type=jnp.float32)

    mixed_near, mixed_far, (attended,) = scattered(out_term, width, (attended,))
    layer_out = (
        x_part.astype(jnp.float32) + mixed_near + mixed_far.astype(jnp.float32)
    ).astype(jnp.bfloat16)
    d_attended = dot(dy_all, wo_dev, NT).astype(jnp.bfloat16)
    d_queries, d_keys, d_values = attend_backward(
        queries, keys, values, attended, d_attended, probs
    )
    pair = jnp.concatenate([d_keys, d_values], axis=1).astype(jnp.bfloat16)
    pairs = lax.all_gather(pair, "tp", axis=1, tiled=True)
    kv_width = wkv_dev.shape[1]
    half = KEY_VALUE_HEADS // 2
    first_kv = 2 * HEAD_SIZE * half * (me % 2) + HEAD_SIZE * (me // 2)
    d_kv_mine = jnp.concatenate(
        [
            lax.dynamic_slice_in_dim(pairs, first_kv + 2 * HEAD_SIZE * g, HEAD_SIZE, 1)
            for g in range(half)
        ],
        axis=1,
    )
    grad_query = dot(normed_all, d_queries, TN).astype(jnp.bfloat16)
    d_kv_mine, d_queries, grad_query = lax.optimization_barrier((d_kv_mine, d_queries, grad_query))

    def in_term(first, d_queries, d_kv_mine, *later):
        block = lax.dynamic_slice_in_dim(wq_dev, first, width, 0)
        kv_block = lax.dynamic_slice_in_dim(wkv_dev, first, width, 0)
        return dot(d_queries, block, NT) + dot(d_kv_mine, kv_block, NT)

    d_near, d_far, (d_queries, d_kv_mine, attended, normed_all) = scattered(
        in_term, width, (d_queries, d_kv_mine, attended, normed_all)
    )
    grad_out = dot(attended, dy_all, TN).astype(jnp.bfloat16)
    grad_keyval = dot(normed_all, d_kv_mine, TN).astype(jnp.bfloat16)

    def product(a, b):
        return jnp.sum(a.astype(jnp.float32) * b.astype(jnp.float32), axis=1)

    row_dot = product(d_queries, queries) + product(
        pair, jnp.concatenate([keys, values], axis=1)
    )
    row_dot = jnp.sum(lax.all_gather(row_dot, "tp"), axis=0)
    row_mean = (row_dot / features)[:, None]
    gain_mine = lax.dynamic_slice_in_dim(gain_row, mine, width, 0)
    unit_mine = x_part.astype(jnp.float32) * inv_rms
    d_normed = d_near + d_far.astype(jnp.float32)
    grad_gain = lax.all_gather(jnp.sum(d_normed * unit_mine, axis=0), "tp", tiled=True)
    d_unit = d_normed * gain_mine
    grad_in = (
        dy_part.astype(jnp.float32) + inv_rms * (d_unit - unit_mine * row_mean)
    ).astype(jnp.bfloat16)
    return (
        layer_out[None],
        grad_in[None],
        grad_query[None],
        grad_keyval[None],
        grad_out[None],
        grad_gain[None],
    )


def on_device_any(x_handed, cot_handed, w_query, key_value_weight, w_out, norm_gain):
    x_part = shifted(x_handed, "section", 1)[0]
    dy_part = shifted(cot_handed, "section", -1)[0]
    wq_dev = w_query[0]
    wkv_dev = key_value_weight[0]
    wo_dev = w_out[0]
    gain_row = norm_gain[0]
    heads_per_device = wq_dev.shape[1] // HEAD_SIZE
    score_scale = HEAD_SIZE ** (-0.5)
    x_all = lax.all_gather(x_part, "tp", axis=1, tiled=True)
    sequence_length = x_all.shape[0]
    tok_rows = sequence_length // lax.axis_size("tp")
    row_start = lax.axis_index("tp") * tok_rows
    x_float = x_all.astype(jnp.float32)
    inv_rms = lax.rsqrt(jnp.mean(x_float * x_float, axis=-1, keepdims=True) + 1e-05)
    unit_x = x_float * inv_rms
    normed_all = (unit_x * gain_row).astype(jnp.bfloat16)
    queries = jnp.dot(normed_all, wq_dev, preferred_element_type=jnp.float32).astype(jnp.bfloat16)
    kv_part = jnp.dot(normed_all, wkv_dev, preferred_element_type=jnp.float32).astype(jnp.bfloat16)
    key_value_pairs = lax.all_gather(kv_part, "tp", axis=1, tiled=True)
    key_value_head = lax.axis_index("tp") * heads_per_device // (QUERY_HEADS // KEY_VALUE_HEADS)
    key_rows = lax.dynamic_slice_in_dim(key_value_pairs, key_value_head * HEAD_SIZE, HEAD_SIZE, 1)
    value_rows_full = lax.dynamic_slice_in_dim(
        key_value_pairs, KEY_VALUE_HEADS * HEAD_SIZE + key_value_head * HEAD_SIZE, HEAD_SIZE, 1
    )
    query_heads = queries.reshape(sequence_length, heads_per_device, HEAD_SIZE)
    scores = (
        jnp.einsum("shd,td->hst", query_heads, key_rows, preferred_element_type=jnp.float32)
        * score_scale
    )
    row_ids = lax.broadcasted_iota(jnp.int32, (sequence_length, sequence_length), 0)
    col_ids = lax.broadcasted_iota(jnp.int32, (sequence_length, sequence_length), 1)
    causal = row_ids >= col_ids
    scores = jnp.where(causal[None], scores, jnp.float32(-1e30))
    row_max = jnp.max(scores, axis=-1, keepdims=True)
    shifted_exp = jnp.exp(scores - row_max)
    attn_probs = shifted_exp / jnp.sum(shifted_exp, axis=-1, keepdims=True)
    probs_bf = attn_probs.astype(jnp.bfloat16)
    attended = jnp.einsum(
        "hst,td->shd", probs_bf, value_rows_full, preferred_element_type=jnp.float32
    ).astype(jnp.bfloat16)
    attn_flat = attended.reshape(sequence_length, heads_per_device * HEAD_SIZE)
    out_terms = jnp.dot(attn_flat, wo_dev, preferred_element_type=jnp.float32)
    mixed_part = lax.psum_scatter(
        out_terms.astype(jnp.bfloat16), "tp", scatter_dimension=1, tiled=True
    ).astype(jnp.float32)
    layer_out = (x_part.astype(jnp.float32) + mixed_part).astype(jnp.bfloat16)
    dy_all = lax.all_gather(dy_part, "tp", axis=1, tiled=True)
    grad_out = jnp.einsum(
        "sk,sd->kd", attn_flat, dy_all, preferred_element_type=jnp.float32
    ).astype(jnp.bfloat16)
    d_attended = jnp.einsum("sd,kd->sk", dy_all, wo_dev, preferred_element_type=jnp.float32).astype(
        jnp.bfloat16
    )
    d_att_heads = d_attended.reshape(sequence_length, heads_per_device, HEAD_SIZE)
    d_probs = jnp.einsum(
        "shd,td->hst", d_att_heads, value_rows_full, preferred_element_type=jnp.float32
    )
    row_delta = jnp.einsum(
        "shd,shd->hs", d_att_heads.astype(jnp.float32), attended.astype(jnp.float32)
    )
    d_scores = (attn_probs * (d_probs - row_delta[:, :, None]) * score_scale).astype(jnp.bfloat16)
    d_queries = jnp.einsum("hst,td->shd", d_scores, key_rows, preferred_element_type=jnp.float32)
    d_queries = d_queries.astype(jnp.bfloat16).reshape(
        sequence_length, heads_per_device * HEAD_SIZE
    )
    d_key_rows = jnp.einsum(
        "hst,shd->td", d_scores, query_heads, preferred_element_type=jnp.float32
    )
    value_row_gradient = jnp.einsum(
        "hst,shd->td", probs_bf, d_att_heads, preferred_element_type=jnp.float32
    )
    key_value_contribution = jnp.zeros(
        (sequence_length, 2 * KEY_VALUE_HEADS * HEAD_SIZE), jnp.float32
    )
    key_value_contribution = lax.dynamic_update_slice(
        key_value_contribution, d_key_rows, (jnp.int32(0), key_value_head * HEAD_SIZE)
    )
    key_value_contribution = lax.dynamic_update_slice(
        key_value_contribution,
        value_row_gradient,
        (jnp.int32(0), KEY_VALUE_HEADS * HEAD_SIZE + key_value_head * HEAD_SIZE),
    )
    d_keyvals = lax.psum_scatter(
        key_value_contribution.astype(jnp.bfloat16), "tp", scatter_dimension=1, tiled=True
    )
    grad_query = jnp.einsum(
        "sd,sk->dk", normed_all, d_queries, preferred_element_type=jnp.float32
    ).astype(jnp.bfloat16)
    grad_keyval = jnp.einsum(
        "sd,sk->dk", normed_all, d_keyvals, preferred_element_type=jnp.float32
    ).astype(jnp.bfloat16)
    from_query = jnp.einsum("sk,dk->sd", d_queries, wq_dev, preferred_element_type=jnp.float32)
    from_keyval = jnp.einsum("sk,dk->sd", d_keyvals, wkv_dev, preferred_element_type=jnp.float32)
    d_normed = lax.psum_scatter(
        (from_query + from_keyval).astype(jnp.bfloat16), "tp", scatter_dimension=0, tiled=True
    ).astype(jnp.float32)
    unit_rows = lax.dynamic_slice_in_dim(unit_x, row_start, tok_rows, 0)
    inv_rows = lax.dynamic_slice_in_dim(inv_rms, row_start, tok_rows, 0)
    dy_rows = lax.dynamic_slice_in_dim(dy_all, row_start, tok_rows, 0).astype(jnp.float32)
    gain_local = jnp.sum(d_normed * unit_rows, axis=0)
    grad_gain = lax.psum(gain_local, "tp")
    d_unit = d_normed * gain_row
    d_input = inv_rows * (d_unit - unit_rows * jnp.mean(d_unit * unit_rows, axis=-1, keepdims=True))
    grad_rows = (dy_rows + d_input).astype(jnp.bfloat16)
    grad_in = lax.all_to_all(grad_rows, "tp", split_axis=1, concat_axis=0, tiled=True)
    return (
        layer_out[None],
        grad_in[None],
        grad_query[None],
        grad_keyval[None],
        grad_out[None],
        grad_gain[None],
    )


def solution(mesh):
    return jax.shard_map(
        on_device if mesh.shape["tp"] == KEY_VALUE_HEADS else on_device_any,
        mesh=mesh,
        in_specs=(
            P("section", None, "tp"),
            P("section", None, "tp"),
            P("section", None, "tp"),
            P("section", None, "tp"),
            P("section", "tp", None),
            P("section", None),
        ),
        out_specs=(
            P("section", None, "tp"),
            P("section", None, "tp"),
            P("section", None, "tp"),
            P("section", None, "tp"),
            P("section", "tp", None),
            P("section", None),
        ),
        check_vma=False,
    )
```
